32 devices in a mesh: px: 8 (over y, x, core), py: 4 (over z).
Axes of the slice: x: 2, y: 2, z: 4, core: 2. Of those that a mesh axis runs over, the one named last changes fastest.
Arguments:
- node_latents: bfloat16 [128, 80, 512], P('px', 'py'), may hold values from -6 to 6
- fine_edges: bfloat16 [128, 80, 6, 512], P('px', 'py'), may hold values from -6 to 6
- long_edges: bfloat16 [5120, 512], P(('px', 'py')), may hold values from -6 to 6
- neighbours: int32 [128, 80, 6], P('px', 'py'), may hold values from 0 to 7, as said below
- coarse_slots: int32 [640], P(('px', 'py')), may hold values from 0 to 319, as said below
- long_senders: int32 [5120], P(('px', 'py')), may hold values from 0 to 639
- long_receivers: int32 [5120], P(('px', 'py')), may hold values from 0 to 639, as said below
- edge_inner: bfloat16 [2, 1536, 512], replicated, may hold values from -0.15625 to 0.15625
- edge_outer: bfloat16 [2, 512, 512], replicated, may hold values from -0.25 to 0.25
- edge_gain: float32 [2, 512], replicated, may hold values from 0.5 to 1.5
- node_inner: bfloat16 [2, 1024, 512], replicated, may hold values from -0.1875 to 0.1875
- node_outer: bfloat16 [2, 512, 512], replicated, may hold values from -0.25 to 0.25
- node_gain: float32 [2, 512], replicated, may hold values from 0.5 to 1.5
Outputs:
- new_nodes: bfloat16 [128, 80, 512], P('px', 'py')
- new_fine: bfloat16 [128, 80, 6, 512], P('px', 'py')
- new_long: bfloat16 [5120, 512], P(('px', 'py'))
The draws below stay inside these ranges and needn't reach their ends.
Inputs may be any that keep to these rules, and one draw needn't show every extreme that they name: `neighbours`: the 6 codes of one node are different. `coarse_slots`: the 20 entries of one device's block are different. `long_receivers`: among the 160 long edges of one device, at most 10 have receivers c with the same c // 20, and on every device some such group has exactly 10.
All inputs are finite; a program needn't handle non-finite values.
Results may differ from the reference program's by a relative error of at most 0.0095.
Values may be sent and summed in bfloat16 or wider, within the bound.
A program may use at most 128 MiB of HBM per device.

```python
import jax
import jax.numpy as jnp
from jax import lax

D = 512
HID = 512
K = 6
LAYERS = 2
PR = 16
PC = 20
CO_DEV = 20
LE_DEV = 160
GR = 128
GC = 80
COARSE = 640
LONG = 5120
CAP = 10
N_PY = 4


def draw_neighbours(key, part):
    scores = jax.random.randint(key, (GR, GC, 8), 0, 1 << 20) * 8 + jnp.arange(8, dtype=jnp.int32)
    ranking = jnp.argsort(scores, axis=-1, stable=True)
    return ranking[..., :K].astype(jnp.int32)


def draw_coarse_slots(key, part):
    patch_cells = PR * PC
    blocks = COARSE // CO_DEV
    scores = jax.random.randint(key, (blocks, patch_cells), 0, (1 << 30) // patch_cells) * patch_cells + jnp.arange(patch_cells, dtype=jnp.int32)
    ranking = jnp.argsort(scores, axis=-1, stable=True)
    return ranking[:, :CO_DEV].reshape(COARSE).astype(jnp.int32)


def draw_long_receivers(key, part):
    blocks = LONG // LE_DEV
    slot_count = blocks * CAP
    first_key, second_key, third_key, fourth_key = jax.random.split(key, 4)
    favoured = jax.random.randint(first_key, (blocks, 1), 0, blocks)
    positions = jnp.arange(slot_count, dtype=jnp.int32)
    owner_of = positions // CAP
    noise = jax.random.randint(second_key, (blocks, slot_count), 0, (1 << 30) // slot_count)
    scores = jnp.where(owner_of[None, :] == favoured, positions[None, :], (noise + 1) * slot_count + positions[None, :])
    chosen = jnp.argsort(scores, axis=-1, stable=True)[:, :LE_DEV].astype(jnp.int32)
    owners = chosen // CAP
    within = jax.random.randint(third_key, (blocks, LE_DEV), 0, CO_DEV)
    mixing = jax.random.randint(fourth_key, (blocks, LE_DEV), 0, 1 << 20) * LE_DEV + jnp.arange(LE_DEV, dtype=jnp.int32)
    shuffle = jnp.argsort(mixing, axis=-1, stable=True)
    receivers = jnp.take_along_axis(owners * CO_DEV + within, shuffle, axis=1)
    return receivers.reshape(LONG).astype(jnp.int32)


def place_ends(drawn, key, least, top_value):
    longest = drawn.shape.index(max(drawn.shape))
    spots = []
    for shift in (0, 1):
        where = [jax.random.randint(jax.random.fold_in(key, axis), (), 0, length) for axis, length in enumerate(drawn.shape)]
        where[longest] = (where[longest] + shift) % drawn.shape[longest]
        spots.append(tuple(where))
    return drawn.at[spots[0]].set(least).at[spots[1]].set(top_value)


def shard_levels(stream_key, dims, pieces, smallest, largest):
    def one(dim, blocks):
        draws = jax.random.uniform(jax.random.fold_in(jax.random.fold_in(stream_key, 6), dim), (blocks,), jnp.float32, smallest / len(pieces), largest / len(pieces))
        return jnp.repeat(jnp.exp(draws), dims[dim] // blocks).reshape((-1,) + (1,) * (len(dims) - dim - 1))

    loudness = one(*pieces[0])
    for cut in pieces[1:]:
        loudness = loudness * one(*cut)
    return loudness


def normal_values(key, shape, scale, bound, cuts=(), held_as=jnp.bfloat16):
    entries = jax.random.normal(key, shape, jnp.float32) * scale
    if len(cuts) > 0:
        entries = shard_levels(key, shape, cuts, -0.22, 0.18) * entries
    return jnp.clip(entries, min=-bound, max=bound).astype(held_as)


def setup_inputs(seed: int = 0) -> dict:
    streams_of = jax.random.split(jax.random.key(seed), 14)
    return {
        "node_latents": normal_values(streams_of[0], (GR, GC, D), 1.0, 6.0, ((0, 8), (1, 4))),
        "fine_edges": normal_values(streams_of[1], (GR, GC, K, D), 1.0, 6.0, ((0, 8), (1, 4))),
        "long_edges": normal_values(streams_of[2], (LONG, D), 1.0, 6.0, ((0, 32),)),
        "neighbours": draw_neighbours(jax.random.fold_in(streams_of[13], 71), 0),
        "coarse_slots": draw_coarse_slots(jax.random.fold_in(streams_of[13], 71), 0),
        "long_senders": place_ends(jax.random.randint(streams_of[5], (LONG,), 0, COARSE), jax.random.fold_in(streams_of[5], 1), 0, COARSE - 1).astype(jnp.int32),
        "long_receivers": draw_long_receivers(jax.random.fold_in(streams_of[13], 71), 0),
        "edge_inner": normal_values(streams_of[7], (LAYERS, 3 * D, HID), (3 * D) ** -0.5, 0.15625),
        "edge_outer": normal_values(streams_of[8], (LAYERS, HID, D), HID ** -0.5, 0.25),
        "edge_gain": jnp.clip(1.0 + 0.1 * jax.random.normal(streams_of[9], (LAYERS, D), jnp.float32), 0.5, 1.5),
        "node_inner": normal_values(streams_of[10], (LAYERS, 2 * D, HID), (2 * D) ** -0.5, 0.1875),
        "node_outer": normal_values(streams_of[11], (LAYERS, HID, D), HID ** -0.5, 0.25),
        "node_gain": jnp.clip(1.0 + 0.1 * jax.random.normal(streams_of[12], (LAYERS, D), jnp.float32), 0.5, 1.5),
    }


EPSILON = 1e-05

def layer_norm(values, gains):
    center = values - lax.optimization_barrier(jnp.mean(values, axis=-1, keepdims=True))
    spread = lax.optimization_barrier(jnp.mean(center * center, axis=-1, keepdims=True))
    return center * lax.rsqrt(spread + EPSILON) * gains

def apply_mlp(inputs, before, inner, outer, gains):
    hidden = jax.nn.silu(jnp.dot(inputs, inner, preferred_element_type=jnp.float32)).astype(jnp.bfloat16)
    output = jnp.dot(hidden, outer, preferred_element_type=jnp.float32)
    return (before.astype(jnp.float32) + layer_norm(output, gains)).astype(jnp.bfloat16)

def reference(node_latents, fine_edges, long_edges, neighbours, coarse_slots, long_senders, long_receivers, edge_inner, edge_outer, edge_gain, node_inner, node_outer, node_gain):
    grid_rows, grid_columns, features = node_latents.shape
    shifted_code = neighbours + (neighbours >= 4).astype(jnp.int32)
    rows_here = lax.broadcasted_iota(jnp.int32, neighbours.shape, 0)
    cols_here = lax.broadcasted_iota(jnp.int32, neighbours.shape, 1)
    sender_rows = (rows_here + shifted_code // 3 - 1) % grid_rows
    sender_cols = (cols_here + shifted_code % 3 - 1) % grid_columns
    sender_flat = (sender_rows * grid_columns + sender_cols).reshape(-1).astype(jnp.int32)
    owner_device = lax.iota(jnp.int32, COARSE) // CO_DEV
    coarse_row = owner_device // N_PY * PR + coarse_slots // PC
    coarse_col = owner_device % N_PY * PC + coarse_slots % PC
    coarse_flat = (coarse_row * grid_columns + coarse_col).astype(jnp.int32)
    grid_cells = grid_rows * grid_columns
    latents = node_latents.reshape(grid_cells, features)
    fine_rows = fine_edges.reshape(grid_cells * K, features)
    long_rows = long_edges
    for layer_index in range(LAYERS):
        receivers_here = jnp.repeat(latents, K, axis=0)
        inputs = jnp.concatenate([fine_rows, jnp.take(latents, sender_flat, axis=0), receivers_here], axis=1)
        fine_rows = apply_mlp(inputs, fine_rows, edge_inner[layer_index], edge_outer[layer_index], edge_gain[layer_index])
        coarse = jnp.take(latents, coarse_flat, axis=0)
        long_inputs = jnp.concatenate([long_rows, jnp.take(coarse, long_senders, axis=0), jnp.take(coarse, long_receivers, axis=0)], axis=1)
        long_rows = apply_mlp(long_inputs, long_rows, edge_inner[layer_index], edge_outer[layer_index], edge_gain[layer_index])
        incoming = lax.optimization_barrier(jnp.sum(fine_rows.reshape(grid_cells, K, features).astype(jnp.float32), axis=1))
        long_totals = jax.ops.segment_sum(long_rows.astype(jnp.float32), long_receivers, num_segments=COARSE)
        incoming = incoming.at[coarse_flat].add(long_totals).astype(jnp.bfloat16)
        node_inputs = jnp.concatenate([latents, incoming], axis=1)
        latents = apply_mlp(node_inputs, latents, node_inner[layer_index], node_outer[layer_index], node_gain[layer_index])
    return (latents.reshape(node_latents.shape), fine_rows.reshape(fine_edges.shape), long_rows)
```

```python
import functools

import jax
import jax.numpy as jnp
import numpy as np
from jax import lax
from jax.experimental import pallas as pl
from jax.experimental.pallas import tpu as pltpu
from jax.sharding import PartitionSpec as P

EPSILON = 1e-05
MESH = pl.DeviceIdType.MESH
BF = jnp.bfloat16
F32 = jnp.float32


def up16(count):
    return -(-count // 16) * 16


def dot(a, b):
    return jnp.dot(a, b, preferred_element_type=F32)


def onehot(index, shape, axis):
    return jnp.where(lax.broadcasted_iota(jnp.int32, shape, axis) == index, 1.0, 0.0).astype(BF)


def finish(before, inner_sum, outer, gains):
    hidden = (0.5 * inner_sum * (1.0 + jnp.tanh(0.5 * inner_sum))).astype(BF)
    output = dot(hidden, outer)
    center = output - jnp.mean(output, axis=-1, keepdims=True)
    spread = jnp.mean(center * center, axis=-1, keepdims=True)
    return (before.astype(F32) + center * lax.rsqrt(spread + EPSILON) * gains).astype(BF)


def kernel(
    rows, columns, counts, block,
    lat_ref, fine_ref, long_ref, sidx_ref, pidx_ref, cols_ref, place_ref, slots_ref,
    eg_ref, ng_ref, ei_hbm, eo_hbm, ni_hbm, no_hbm,
    nodes_out, fine_out, long_out,
    h_ref, onehots, spread_ref, recv_terms, incoming, select_ref,
    send_buf, source, coarse, bucket, arrived, labels_out, labels_in,
    ei, eo, ni, no,
    w_sem, halo_send, halo_recv, coarse_send, coarse_recv,
    bucket_send, bucket_recv, label_send, label_recv,
):
    npx, npy = counts
    devices = npx * npy
    cells, features = lat_ref.shape
    degree = fine_ref.shape[1]
    layers = ei.shape[0]
    cslots = up16(slots_ref.shape[1])
    x, y = lax.axis_index("px"), lax.axis_index("py")
    me = x * npy + y
    down, up = lax.rem(x + 1, npx), lax.rem(x + npx - 1, npx)
    right, left = lax.rem(y + 1, npy), lax.rem(y + npy - 1, npy)
    wr, hr = up16(columns), up16(rows)
    sizes = (wr, wr, hr, hr, 16, 16, 16, 16)
    offsets = tuple(int(v) for v in np.cumsum((0,) + sizes))
    halo = offsets[-1]
    targets = (
        (down, y), (up, y), (x, right), (x, left),
        (down, right), (down, left), (up, right), (up, left),
    )

    loads = []
    for layer in range(layers):
        for j, (src, dst) in enumerate(((ei_hbm, ei), (eo_hbm, eo), (ni_hbm, ni), (no_hbm, no))):
            copy = pltpu.make_async_copy(src.at[layer], dst.at[layer], w_sem.at[layer, j])
            copy.start()
            loads.append(copy)

    def place(base, size):
        return pl.ds(pl.multiple_of(base * size, size), size)

    def to_all(src_of, dst, send_sem, recv_sem):
        def send(i, carry):
            peer = lax.rem(me + i, devices)
            pltpu.make_async_remote_copy(
                src_ref=src_of(peer),
                dst_ref=dst,
                send_sem=send_sem,
                recv_sem=recv_sem,
                device_id=(peer // npy, lax.rem(peer, npy)),
                device_id_type=MESH,
            ).start()
            return carry

        lax.fori_loop(1, devices, send, 0)

    def await_all(ref, size, sem):
        part = ref.at[pl.ds(0, size * (devices - 1))]
        pltpu.make_async_copy(part, part, sem).wait()

    def start_exchange(layer):
        h = h_ref[...]
        picked = dot(onehot(pidx_ref[...], (halo + cslots, cells), 1), h).astype(BF)
        send_buf[layer] = picked
        source[layer, pl.ds(0, cells)] = h
        coarse[layer, place(me, cslots)] = picked[halo:]
        copies = []
        for j, target in enumerate(targets):
            copy = pltpu.make_async_remote_copy(
                src_ref=send_buf.at[layer, pl.ds(offsets[j], sizes[j])],
                dst_ref=source.at[layer, pl.ds(cells + offsets[j], sizes[j])],
                send_sem=halo_send.at[layer, j],
                recv_sem=halo_recv.at[layer, j],
                device_id=target,
                device_id_type=MESH,
            )
            copy.start()
            copies.append(copy)
        to_all(
            lambda peer: send_buf.at[layer, pl.ds(halo, cslots)],
            coarse.at[layer, place(me, cslots)],
            coarse_send.at[layer],
            coarse_recv.at[layer],
        )
        return copies

    h_ref[...] = lat_ref[...]
    copies = start_exchange(0)
    placing = onehot(place_ref[...], (devices * block, long_ref.shape[0]), 0)
    tags = jnp.broadcast_to(cols_ref[:, 2:3].astype(F32), (long_ref.shape[0], 128)).astype(BF)
    labels_out[...] = dot(placing, tags).astype(BF)
    labels_in[place(me, block)] = labels_out[place(me, block)]
    to_all(
        lambda peer: labels_out.at[place(peer, block)],
        labels_in.at[place(me, block)],
        label_send.at[0],
        label_recv.at[0],
    )

    group = 16

    def regroup(i, carry):
        base = pl.multiple_of(i * group, group)
        taken = fine_ref[pl.ds(base, group)].astype(F32)
        for q in range(features // 128):
            lanes = slice(128 * q, 128 * q + 128)
            for j in range(group):
                spread_ref[q, pl.ds(8 * j, degree), :] = taken[j][:, lanes]
        for k in range(degree):
            for q in range(features // 128):
                lanes = slice(128 * q, 128 * q + 128)
                fine_out[k, pl.ds(base, group), lanes] = spread_ref.at[q][
                    pl.ds(k, group, stride=8), :
                ].astype(BF)
        return carry

    lax.fori_loop(0, cells // group, regroup, 0)
    for k in range(degree):
        onehots[k] = onehot(sidx_ref[:, k : k + 1], (cells, cells + halo), 1)
    long_out[...] = long_ref[...]

    for layer in range(layers):
        for j in range(4):
            loads[4 * layer + j].wait()
        if layer > 0:
            copies = start_exchange(layer)
        edge_part = ei.at[layer, pl.ds(0, features)]
        send_part = ei.at[layer, pl.ds(features, features)]
        receive_part = ei.at[layer, pl.ds(2 * features, features)]
        gains = eg_ref[layer : layer + 1, :]
        recv_terms[...] = dot(h_ref[...], receive_part[...])
        incoming[...] = jnp.zeros_like(incoming)
        for copy in copies:
            copy.wait()
        terms = dot(source[layer], send_part[...]).astype(BF)
        source[layer] = terms

        def fine(k, carry):
            before = fine_out[k]
            inner = dot(before, edge_part[...]) + dot(onehots[k], source[layer]) + recv_terms[...]
            after = finish(before, inner, eo[layer], gains)
            fine_out[k] = after
            incoming[...] += after.astype(F32)
            return carry

        lax.fori_loop(0, degree // 2, fine, 0)

        await_all(coarse.at[layer], cslots, coarse_recv.at[layer])
        table = coarse[layer]
        long_count = long_ref.shape[0]
        wide = (long_count, devices * cslots)
        from_rows = dot(onehot(cols_ref[:, 0:1], wide, 1), table).astype(BF)
        to_rows = dot(onehot(cols_ref[:, 1:2], wide, 1), table).astype(BF)
        before = long_out[...]
        inner = dot(before, edge_part[...])
        inner = inner + dot(from_rows, send_part[...])
        inner = inner + dot(to_rows, receive_part[...])
        after = finish(before, inner, eo[layer], gains)
        long_out[...] = after
        bucket[layer] = dot(
            onehot(place_ref[...], (devices * block, long_count), 0), after
        ).astype(BF)
        arrived[layer, place(me, block)] = bucket[layer, place(me, block)]
        to_all(
            lambda peer: bucket.at[layer, place(peer, block)],
            arrived.at[layer, place(me, block)],
            bucket_send.at[layer],
            bucket_recv.at[layer],
        )

        lax.fori_loop(degree // 2, degree, fine, 0)

        if layer == 0:
            await_all(labels_in, block, label_recv.at[0])
            names = labels_in[:, 0:1].astype(F32)
            lane = lax.broadcasted_iota(jnp.int32, (devices * block, cslots), 1).astype(F32)
            chooser = jnp.where(lane + 1.0 == names, 1.0, 0.0).astype(BF)
            owner = onehot(slots_ref[...], (cells, cslots), 0)
            select_ref[...] = lax.dot_general(
                owner, chooser, (((1,), (1,)), ((), ())), preferred_element_type=F32
            ).astype(BF)
        h = h_ref[...]
        inner = dot(h, ni[layer, pl.ds(0, features)])
        await_all(arrived.at[layer], block, bucket_recv.at[layer])
        total = (incoming[...] + dot(select_ref[...], arrived[layer])).astype(BF)
        inner = inner + dot(total, ni[layer, pl.ds(features, features)])
        h_ref[...] = finish(h, inner, no[layer], ng_ref[layer : layer + 1, :])

    nodes_out[...] = h_ref[...]
    await_all(labels_out, block, label_send.at[0])
    for layer in range(layers):
        await_all(coarse.at[layer], cslots, coarse_send.at[layer])
        await_all(bucket.at[layer], block, bucket_send.at[layer])


def sender_slots(neighbours, rows, columns):
    cells, degree = rows * columns, neighbours.shape[-1]
    code = neighbours + (neighbours >= 4).astype(jnp.int32)
    r = lax.broadcasted_iota(jnp.int32, neighbours.shape, 0) + code // 3 - 1
    c = lax.broadcasted_iota(jnp.int32, neighbours.shape, 1) + code % 3 - 1
    wr, hr = up16(columns), up16(rows)
    corner = cells + 2 * wr + 2 * hr
    top, bottom, west, east = r < 0, r >= rows, c < 0, c >= columns
    middle = jnp.where(west, cells + 2 * wr + r, jnp.where(east, cells + 2 * wr + hr + r, r * columns + c))
    above = jnp.where(west, corner, jnp.where(east, corner + 16, cells + c))
    below = jnp.where(west, corner + 32, jnp.where(east, corner + 48, cells + wr + c))
    return jnp.where(top, above, jnp.where(bottom, below, middle)).reshape(cells, degree)


def shards(
    counts,
    node_latents, fine_edges, long_edges, neighbours, coarse_slots, long_senders, long_receivers,
    edge_inner, edge_outer, edge_gain, node_inner, node_outer, node_gain,
):
    rows, columns, features = node_latents.shape
    degree = fine_edges.shape[2]
    hidden = edge_inner.shape[2]
    coarse_count = coarse_slots.shape[0]
    long_count = long_edges.shape[0]
    layers = edge_inner.shape[0]
    devices = counts[0] * counts[1]
    cells = rows * columns
    capacity = (2 * long_count + devices - 1) // devices
    block = up16(capacity)
    cslots = up16(coarse_count)

    wr, hr = up16(columns), up16(rows)
    cell = np.arange(cells).reshape(rows, columns)
    fixed = []
    for part, size in (
        (cell[-1], wr), (cell[0], wr), (cell[:, -1], hr), (cell[:, 0], hr),
        (cell[-1:, -1], 16), (cell[-1:, 0], 16), (cell[:1, -1], 16), (cell[:1, 0], 16),
    ):
        fixed.append(np.concatenate([part, np.full(size - len(part), -1)]))
    fixed = np.concatenate(fixed).astype(np.int32)
    halo = len(fixed)
    padded_slots = jnp.pad(coarse_slots, (0, cslots - coarse_count), constant_values=-1)
    pidx = jnp.concatenate([jnp.asarray(fixed), padded_slots])[:, None]

    owners = long_receivers // coarse_count
    within = long_receivers - owners * coarse_count
    earlier = lax.broadcasted_iota(jnp.int32, (long_count, long_count), 0) < lax.broadcasted_iota(
        jnp.int32, (long_count, long_count), 1
    )
    ranking = jnp.sum(
        ((owners[:, None] == owners[None, :]) & earlier).astype(jnp.int32), axis=0
    )
    placed = (owners * block + ranking)[None, :]
    from_owner = long_senders // coarse_count
    cols = jnp.stack(
        [
            from_owner * cslots + (long_senders - from_owner * coarse_count),
            owners * cslots + within,
            within + 1,
        ],
        axis=1,
    )
    vmem = pl.BlockSpec(memory_space=pltpu.VMEM)
    hbm = pl.BlockSpec(memory_space=pltpu.HBM)
    dma = pltpu.SemaphoreType.DMA
    nodes, fine, long_rows = pl.pallas_call(
        functools.partial(kernel, rows, columns, counts, block),
        out_shape=(
            jax.ShapeDtypeStruct((cells, features), BF),
            jax.ShapeDtypeStruct((degree, cells, features), BF),
            jax.ShapeDtypeStruct((long_count, features), BF),
        ),
        in_specs=[vmem] * 10 + [hbm] * 4,
        out_specs=(vmem, vmem, vmem),
        scratch_shapes=[
            pltpu.VMEM((cells, features), BF),
            pltpu.VMEM((degree, cells, cells + halo), BF),
            pltpu.VMEM((features // 128, 128, 128), F32),
            pltpu.VMEM((cells, hidden), F32),
            pltpu.VMEM((cells, features), F32),
            pltpu.VMEM((cells, devices * block), BF),
            pltpu.VMEM((layers, halo + cslots, features), BF),
            pltpu.VMEM((layers, cells + halo, features), BF),
            pltpu.VMEM((layers, devices * cslots, features), BF),
            pltpu.VMEM((layers, devices * block, features), BF),
            pltpu.VMEM((layers, devices * block, features), BF),
            pltpu.VMEM((devices * block, 128), BF),
            pltpu.VMEM((devices * block, 128), BF),
            pltpu.VMEM(edge_inner.shape, BF),
            pltpu.VMEM(edge_outer.shape, BF),
            pltpu.VMEM(node_inner.shape, BF),
            pltpu.VMEM(node_outer.shape, BF),
            dma((layers, 4)),
            dma((layers, 8)),
            dma((layers, 8)),
            dma((layers,)),
            dma((layers,)),
            dma((layers,)),
            dma((layers,)),
            dma((1,)),
            dma((1,)),
        ],
        compiler_params=pltpu.CompilerParams(
            has_side_effects=True, vmem_limit_bytes=62 * 1024 * 1024
        ),
    )(
        node_latents.reshape(cells, features),
        fine_edges.reshape(cells, degree, features),
        long_edges,
        sender_slots(neighbours, rows, columns),
        pidx,
        cols,
        placed,
        padded_slots[None, :],
        edge_gain,
        node_gain,
        edge_inner,
        edge_outer,
        node_inner,
        node_outer,
    )
    return (
        nodes.reshape(node_latents.shape),
        jnp.transpose(fine, (1, 0, 2)).reshape(fine_edges.shape),
        long_rows,
    )


def solution(mesh):
    in_specs = (
        P("px", "py", None),
        P("px", "py", None, None),
        P(("px", "py"), None),
        P("px", "py", None),
        P(("px", "py")),
        P(("px", "py")),
        P(("px", "py")),
        P(),
        P(),
        P(),
        P(),
        P(),
        P(),
    )
    out_specs = (P("px", "py", None), P("px", "py", None, None), P(("px", "py"), None))
    counts = (mesh.shape["px"], mesh.shape["py"])
    return jax.shard_map(
        functools.partial(shards, counts),
        mesh=mesh,
        in_specs=in_specs,
        out_specs=out_specs,
        check_vma=False,
    )
```
